1024 devices in a mesh: pipe: 16 (over z_lo), ctx: 8 (over z_hi, x), tp: 8 (over y, core).
Axes of the slice: x: 4, y: 4, z: 32 (z_hi: 2, z_lo: 16; z = z_hi * 16 + z_lo), core: 2. Of those that a mesh axis runs over, the one named last changes fastest.
Arguments:
- inputs: bfloat16 [16, 2048, 5120], P('pipe', ('ctx', 'tp')), may hold values from -6 to 6
- doc_lengths: int32 [16, 8], P('pipe'), may hold values from 1 to 1024, 2048 in all within a row
- w_query: bfloat16 [16, 5120, 3072], P('pipe', None, 'tp'), may hold values from -0.078125 to 0.078125
- w_key: bfloat16 [16, 5120, 1024], P('pipe', 'ctx', 'tp'), may hold values from -0.078125 to 0.078125
- w_value: bfloat16 [16, 5120, 1024], P('pipe', 'ctx', 'tp'), may hold values from -0.078125 to 0.078125
- w_out: bfloat16 [16, 3072, 5120], P('pipe', 'tp'), may hold values from -0.625 to 0.625
Outputs:
- next_input: bfloat16 [16, 2048, 5120], P('pipe', ('ctx', 'tp'))
The draws below stay inside these ranges and needn't reach their ends.
Inputs may be any that keep to these rules, and one draw needn't show every extreme that they name: `doc_lengths`: the 8 lengths of a micro-batch sum to 2048; the longest is exactly 1024.
All inputs are finite; a program needn't handle non-finite values.
Results may differ from the reference program's by a relative error of at most 0.015.
Values may be sent and summed in bfloat16 or wider, within the bound.
A program may use at most 64 MiB of HBM per device.

```python
import math
import jax
import jax.numpy as jnp
import numpy as np
from jax import lax

D = 5120
KH = 8
HD = 128
QH = 24
TOK_DEV = 256
SPAN = 1024
DOCS = 8
L = 2048
SECTIONS = 16
N_TP = 8


def steps_of(own_key, shape, split, least, high):
    factor_of = 1.0
    for axis_at, blocks in split:
        steps = jax.random.uniform(jax.random.fold_in(jax.random.fold_in(own_key, 6), axis_at), (blocks,), jnp.float32, least / len(split), high / len(split))
        factor_of = factor_of * jnp.repeat(jnp.exp(steps), shape[axis_at] // blocks).reshape((-1,) + (1,) * (len(shape) - 1 - axis_at))
    return factor_of


def length_profile(count, total, bound, lean):
    weights = [(1 << 20) // math.isqrt(standing ** lean) + 1 for standing in range(2, count + 1)]
    surplus, given = total - bound - (count - 1), [1] * (count - 1)
    while surplus > 0:
        movable = [i for i in range(count - 1) if given[i] < bound]
        mass, budget = sum([weights[i] for i in movable]), surplus
        for i in movable:
            addition = min(bound - given[i], max(1, budget * weights[i] // mass), surplus)
            given[i] = given[i] + addition
            surplus = surplus - addition
    return np.array([bound] + given)


def uneven_parts(key, amount, total, limit, lean):
    if amount == 2:
        one = jax.random.randint(key, (), max(1, total - limit), min(limit, total - 1) + 1)
        return jnp.stack([one, total - one])
    sizes = jnp.asarray(length_profile(amount, total, limit, lean), jnp.int32)
    twos = (amount - 1) // 2
    source_of, receiver = sizes[1:1 + 2 * twos:2], sizes[2:2 + 2 * twos:2]
    margin = jnp.minimum(source_of - 1, limit - receiver)
    moved = jax.random.randint(jax.random.fold_in(key, 1), (twos,), 0, 1 << 20) % (margin + 1)
    sizes = sizes.at[1:1 + 2 * twos:2].set(source_of - moved).at[2:2 + 2 * twos:2].set(receiver + moved)
    return sizes[jax.random.permutation(jax.random.fold_in(key, 2), amount)]


def noise(rng, dims, width, limit, shards=(), kind=jnp.bfloat16):
    values = width * jax.random.normal(rng, dims, jnp.float32)
    if shards:
        values = values * steps_of(rng, dims, shards, -0.22, 0.18)
    return jnp.clip(values, -limit, limit).astype(kind)


def setup_inputs(seed: int = 0) -> dict:
    arg_keys = jax.random.split(jax.random.key(seed), 7)
    inputs = noise(arg_keys[0], (SECTIONS, L, D), 1.0, 6.0, ((0, 16), (1, 64)))
    doc_lengths = jax.vmap(lambda own: uneven_parts(own, DOCS, L, L // 2, 2))(jax.random.split(arg_keys[1], SECTIONS)).reshape((SECTIONS, DOCS)).astype(jnp.int32)
    w_query = noise(arg_keys[2], (SECTIONS, D, QH * HD), D ** -0.5, 0.078125, ((0, 16), (2, 8)))
    w_key = noise(arg_keys[3], (SECTIONS, D, KH * HD), D ** -0.5, 0.078125, ((0, 16), (1, 8), (2, 8)))
    w_value = noise(arg_keys[4], (SECTIONS, D, KH * HD), D ** -0.5, 0.078125, ((0, 16), (1, 8), (2, 8)))
    w_out = noise(arg_keys[5], (SECTIONS, QH * HD, D), (QH * HD // 32) ** -0.5, 0.625, ((0, 16), (1, 8)))
    return dict(inputs=inputs, doc_lengths=doc_lengths, w_query=w_query, w_key=w_key, w_value=w_value, w_out=w_out)


ROPE_BASE = 500000.0
NORM_EPS = 1e-06

def doc_index(positions, lengths):
    doc_ends = jnp.cumsum(lengths)
    return lax.optimization_barrier(jnp.sum((positions[:, None] >= doc_ends[None, :]).astype(jnp.int32), axis=1))

def norm_rotate(entries, positions, head_count, head_width):
    row_count = entries.shape[0]
    shaped = entries.reshape(row_count, head_count, head_width)
    shaped = shaped * lax.rsqrt(lax.optimization_barrier(jnp.mean(shaped * shaped, axis=-1, keepdims=True)) + NORM_EPS)
    half_width = head_width // 2
    frequencies = jnp.power(ROPE_BASE, -(jnp.arange(half_width, dtype=jnp.float32) * 2.0 / head_width))
    angles = positions.astype(jnp.float32)[:, None] * frequencies[None, :]
    cosine = jnp.cos(angles)[:, None, :]
    sine_part = jnp.sin(angles)[:, None, :]
    first_half = shaped[..., :half_width]
    second = shaped[..., half_width:]
    turned = jnp.concatenate([first_half * cosine - second * sine_part, second * cosine + first_half * sine_part], axis=-1)
    return turned.reshape(row_count, head_count * head_width)

def layer_forward(inputs, lengths, w_query, w_key, w_value, w_out):
    seq_len = inputs.shape[0]
    group_size = QH // KH
    positions = jnp.arange(seq_len, dtype=jnp.int32)
    docs = doc_index(positions, lengths)
    queries = jnp.dot(inputs, w_query, preferred_element_type=jnp.float32)
    key_rows = jnp.dot(inputs, w_key, preferred_element_type=jnp.float32)
    value_rows = jnp.dot(inputs, w_value, preferred_element_type=jnp.float32)
    q_round = norm_rotate(queries, positions, QH, HD).astype(jnp.bfloat16).reshape(seq_len, KH, group_size, HD)
    k_round = norm_rotate(key_rows, positions, KH, HD).astype(jnp.bfloat16).reshape(seq_len, KH, HD)
    v_round = value_rows.astype(jnp.bfloat16).reshape(seq_len, KH, HD)
    k_float = k_round.astype(jnp.float32)
    v_float = v_round.astype(jnp.float32)
    score_scale = 1.0 / HD ** 0.5

    def one_block(start_row):
        q_part = lax.dynamic_slice_in_dim(q_round, start_row, TOK_DEV, 0).astype(jnp.float32)
        q_pos = lax.dynamic_slice_in_dim(positions, start_row, TOK_DEV, 0)
        q_doc = lax.dynamic_slice_in_dim(docs, start_row, TOK_DEV, 0)
        scores = jnp.einsum('tkgd,nkd->kgtn', q_part, k_float) * score_scale
        allowed = (positions[None, :] <= q_pos[:, None]) & (docs[None, :] == q_doc[:, None]) & (positions[None, :] // SPAN == q_pos[:, None] // SPAN)
        weights = lax.optimization_barrier(jnp.where(allowed[None, None], jnp.exp(scores), 0.0).astype(jnp.bfloat16))
        weights = weights.astype(jnp.float32)
        numerator = jnp.einsum('kgtn,nkd->tkgd', weights, v_float)
        denominator = lax.optimization_barrier(jnp.sum(weights, axis=-1))
        return (numerator / jnp.transpose(denominator, (2, 0, 1))[..., None]).astype(jnp.bfloat16)
    starts = jnp.arange(seq_len // TOK_DEV, dtype=jnp.int32) * TOK_DEV
    attended = lax.map(one_block, starts).reshape(seq_len, QH * HD)
    share = QH * HD // N_TP

    def add_group(total, group_index):
        attended_part = lax.dynamic_slice_in_dim(attended, group_index * share, share, 1)
        weight_part = lax.dynamic_slice_in_dim(w_out, group_index * share, share, 0)
        product = lax.optimization_barrier(jnp.dot(attended_part, weight_part, preferred_element_type=jnp.float32).astype(jnp.bfloat16))
        return (total + product.astype(jnp.float32), group_index)
    mixed, unused = lax.scan(add_group, jnp.zeros((seq_len, inputs.shape[1]), jnp.float32), jnp.arange(N_TP, dtype=jnp.int32))
    return mixed.astype(jnp.bfloat16)

def section_forward(packed):
    return layer_forward(packed[0], packed[1], packed[2], packed[3], packed[4], packed[5])

def reference(inputs, doc_lengths, w_query, w_key, w_value, w_out):
    outputs = lax.map(section_forward, (inputs, doc_lengths, w_query, w_key, w_value, w_out))
    return jnp.roll(outputs, 1, axis=0)
```

```python
import functools

import jax
import jax.numpy as jnp
import numpy as np
from jax import lax
from jax.experimental import pallas as pl
from jax.experimental.pallas import tpu as pltpu
from jax.sharding import PartitionSpec as P

HD = 128
ROPE_BASE = 500000.0
NORM_EPS = 1e-06
ROWS = 128
PIECES = 4
NEG = -1e30
MESH = pl.DeviceIdType.MESH


def layer_kernel(
    sizes,
    x_ref, len_ref, freq_ref, wq_ref, wk_ref, wv_ref, wo_ref,
    o_ref,
    tok, wq, wo, wk, wv, q_acc, qr, kv_acc, kvb, mask, cosb, sinb, acc, att,
    part, recv_a, pair, recv_b, outb,
    l_sem, z_s, z_r, t_s, t_r, own_s, own_r, fwd_s, fwd_r, kv_s, kv_r,
    a_s, a_r, b_s, b_r, c_s, c_r,
):
    NP, X, Y = sizes
    TP = 2 * Y
    TR, D = x_ref.shape
    TB = TR * TP
    RB = wk_ref.shape[0]
    QW = wq_ref.shape[1]
    G = QW // HD
    NCH = RB // ROWS
    CW = D // PIECES

    pipe, ctx, t = lax.axis_index("pipe"), lax.axis_index("ctx"), lax.axis_index("tp")
    zhi, x = ctx // X, ctx % X
    y, c = t // 2, t % 2

    z_dev = (pipe, (1 - zhi) * X + x, t)
    next_dev = ((pipe + 1) % NP, ctx, t)
    prev_dev = ((pipe + NP - 1) % NP, ctx, t)
    core_dev = (pipe, ctx, y * 2 + 1 - c)

    def flip(i, r, n):
        out = 0
        bit = 1
        while bit < n:
            b = (i // bit) % 2
            out = out + bit * ((1 - b) if (r // bit) % 2 else b)
            bit *= 2
        return out

    def x_dev(xx):
        return (pipe, zhi * X + xx, t)

    def copy(src, dst, ss, rs, dev):
        return pltpu.make_async_remote_copy(
            src_ref=src, dst_ref=dst, send_sem=ss, recv_sem=rs, device_id=dev, device_id_type=MESH
        )

    def rows(start, n):
        return pl.ds(pl.multiple_of(start, n), n)

    mine = ctx * RB
    theirs = ((1 - zhi) * X + x) * RB

    locals_ = [
        pltpu.make_async_copy(x_ref, tok.at[rows(t * TR, TR)], l_sem.at[0]),
        pltpu.make_async_copy(wk_ref, wk.at[rows(mine, ROWS * NCH)], l_sem.at[1]),
        pltpu.make_async_copy(wv_ref, wv.at[rows(mine, ROWS * NCH)], l_sem.at[2]),
        pltpu.make_async_copy(wq_ref, wq, l_sem.at[3]),
        pltpu.make_async_copy(wo_ref, wo, l_sem.at[4]),
    ]
    for cp in locals_:
        cp.start()

    barrier = pltpu.get_barrier_semaphore()
    friends = [z_dev, next_dev, prev_dev]
    friends += [x_dev(flip(x, r, X)) for r in range(1, X)]
    friends += [(pipe, ctx, flip(t, r, TP)) for r in range(1, TP)]
    for dev in friends:
        pl.semaphore_signal(barrier, inc=1, device_id=dev, device_id_type=MESH)
    pl.semaphore_wait(barrier, len(friends))

    def z_copy(j, i, base):
        src = (wk_ref, wv_ref)[i].at[pl.ds(j * ROWS, ROWS)]
        dst = (wk, wv)[i].at[rows(base + j * ROWS, ROWS)]
        return copy(src, dst, z_s.at[j, i], z_r.at[j, i], z_dev)

    for j in range(NCH):
        for i in range(2):
            z_copy(j, i, mine).start()

    def tok_copy(r, who):
        return copy(x_ref, tok.at[rows(who * TR, TR)], t_s.at[r - 1], t_r.at[r - 1], (pipe, ctx, flip(t, r, TP)))

    for r in range(1, TP):
        tok_copy(r, t).start()

    def own_copy(r, i, xx):
        dst = (wk, wv)[i].at[rows((zhi * X + xx) * RB, ROWS * NCH)]
        return copy((wk_ref, wv_ref)[i], dst, own_s.at[r - 1, i], own_r.at[r - 1, i], x_dev(flip(x, r, X)))

    for r in range(1, X):
        for i in range(2):
            own_copy(r, i, x).start()

    first = ctx * TB
    row_pos = lax.broadcasted_iota(jnp.int32, (TB, HD), 0) + first
    angle = row_pos.astype(jnp.float32) * freq_ref[0:1, :]
    cosb[...] = jnp.cos(angle)
    lane = lax.broadcasted_iota(jnp.int32, (TB, HD), 1)
    sine = jnp.sin(angle)
    sinb[...] = jnp.where(lane < HD // 2, -sine, sine)

    n_docs = len_ref.shape[1]
    ends = []
    total = 0
    for m in range(n_docs):
        total = total + len_ref[0, m]
        ends.append(total)
    q_pos = lax.broadcasted_iota(jnp.int32, (TB, TB), 0) + first
    q_doc = sum((q_pos >= e).astype(jnp.int32) for e in ends)
    for d in range(X):
        k_pos = lax.broadcasted_iota(jnp.int32, (TB, TB), 1) + (first - d * TB)
        k_doc = sum((k_pos >= e).astype(jnp.int32) for e in ends)
        mask[d] = jnp.where((k_pos <= q_pos) & (k_doc == q_doc), 0.0, NEG)

    def norm_rotate(head):
        scaled = head * lax.rsqrt(jnp.mean(head * head, axis=-1, keepdims=True) + NORM_EPS)
        return (scaled * cosb[...] + pltpu.roll(scaled, HD // 2, 1) * sinb[...]).astype(jnp.bfloat16)

    locals_[0].wait()
    for r in range(1, TP):
        tok_copy(r, flip(t, r, TP)).wait_recv()
    locals_[3].wait()
    q_acc[...] = jnp.zeros_like(q_acc)
    QK = D // (2 * X)

    def q_step(i, carry):
        s = rows(i * QK, QK)
        q_acc[...] += jnp.dot(tok[:, s], wq[s, :], preferred_element_type=jnp.float32)
        return carry

    lax.fori_loop(0, 2 * X, q_step, 0)
    for h in range(G):
        qr[pl.ds(h * TB, TB), :] = norm_rotate(q_acc[:, h * HD : (h + 1) * HD])

    locals_[1].wait()
    locals_[2].wait()
    for r in range(1, X):
        for i in range(2):
            own_copy(r, i, flip(x, r, X)).wait_recv()
    kv_acc[...] = jnp.zeros_like(kv_acc)

    def kv_add(start, n):
        s = rows(start, n)
        left = tok[:, s]
        kv_acc[0] += jnp.dot(left, wk[s, :], preferred_element_type=jnp.float32)
        kv_acc[1] += jnp.dot(left, wv[s, :], preferred_element_type=jnp.float32)

    def kv_step(i, carry):
        kv_add((zhi * X + i) * RB, ROWS * NCH)
        return carry

    lax.fori_loop(0, X, kv_step, 0)

    def fwd_copy(j, r, i, base):
        ref = (wk, wv)[i].at[rows(base + j * ROWS, ROWS)]
        return copy(ref, ref, fwd_s.at[j, r - 1, i], fwd_r.at[j, r - 1, i], x_dev(flip(x, r, X)))

    def peer_base(r):
        return ((1 - zhi) * X + flip(x, r, X)) * RB

    def take_chunk(j):
        kv_add(theirs + j * ROWS, ROWS)
        for r in range(1, X):
            for i in range(2):
                fwd_copy(j, r, i, peer_base(r)).wait_recv()
            kv_add(peer_base(r) + j * ROWS, ROWS)

    for j in range(NCH):
        for i in range(2):
            z_copy(j, i, theirs).wait_recv()
        for r in range(1, X):
            for i in range(2):
                fwd_copy(j, r, i, theirs).start()
        if j:
            take_chunk(j - 1)
    take_chunk(NCH - 1)

    kvb[0, 0] = norm_rotate(kv_acc[0])
    kvb[0, 1] = kv_acc[1].astype(jnp.bfloat16)

    def kv_copy(d, xx):
        return copy(kvb.at[0], kvb.at[d], kv_s.at[d - 1], kv_r.at[d - 1], x_dev(xx))

    for d in range(1, X):

        @pl.when(x + d < X)
        def _(d=d):
            kv_copy(d, x + d).start()

    scale = 1.0 / HD**0.5
    ones = jnp.ones((TB, HD), jnp.bfloat16)

    def attend(d):
        s = lax.dot_general(
            qr[...], kvb[d, 0], (((1,), (1,)), ((), ())), preferred_element_type=jnp.float32
        )
        s = s.reshape(G, TB, TB) * scale + mask[d][None]
        e = jnp.exp(s).astype(jnp.bfloat16).reshape(G * TB, TB)
        return jnp.dot(
            e, jnp.concatenate([kvb[d, 1], ones], axis=1), preferred_element_type=jnp.float32
        )

    acc[...] = attend(0)
    for d in range(1, X):

        @pl.when(x >= d)
        def _(d=d):
            kv_copy(d, x - d).wait_recv()
            acc[...] += attend(d)

    for h in range(G):
        block = acc[pl.ds(h * TB, TB), :]
        att[:, h * HD : (h + 1) * HD] = (block[:, :HD] / block[:, HD:]).astype(jnp.bfloat16)

    locals_[4].wait()

    def a_copy(k):
        return copy(part.at[k, 1 - c], recv_a.at[k], a_s.at[k], a_r.at[k], core_dev)

    def b_copy(k, r):
        yy = flip(y, r, Y)
        return copy(pair.at[k, yy], recv_b.at[k, r - 1], b_s.at[k, r - 1], b_r.at[k, r - 1], (pipe, ctx, yy * 2 + c))

    def c_copy(k):
        return copy(outb.at[k], o_ref.at[:, rows(k * CW, CW)], c_s.at[k], c_r.at[k], next_dev)

    def project(k, carry):
        product = jnp.dot(
            att[...], wo[:, rows(k * CW, CW)], preferred_element_type=jnp.float32
        ).astype(jnp.bfloat16)
        for who in range(TP):
            part[k, who % 2, who // 2] = product[who * TR : (who + 1) * TR]
        a_copy(k).start()
        return carry

    lax.fori_loop(0, PIECES, project, 0)

    def pair_sum(k, carry):
        a_copy(k).wait_recv()
        pair[k] = (part[k, c].astype(jnp.float32) + recv_a[k].astype(jnp.float32)).astype(jnp.bfloat16)
        for r in range(Y - 1, 0, -1):
            b_copy(k, r).start()
        return carry

    lax.fori_loop(0, PIECES, pair_sum, 0)

    def last_sum(k, carry):
        whole = part[k, c, y].astype(jnp.float32) + recv_a[k, y].astype(jnp.float32)
        for r in range(1, Y):
            b_copy(k, r).wait_recv()
            whole = whole + recv_b[k, r - 1].astype(jnp.float32)
        outb[k] = whole.astype(jnp.bfloat16)
        c_copy(k).start()
        return carry

    lax.fori_loop(0, PIECES, last_sum, 0)

    for j in range(NCH):
        for i in range(2):
            z_copy(j, i, mine).wait_send()
            for r in range(1, X):
                fwd_copy(j, r, i, theirs).wait_send()
    for r in range(1, TP):
        tok_copy(r, t).wait_send()
    for r in range(1, X):
        for i in range(2):
            own_copy(r, i, x).wait_send()
    for d in range(1, X):

        @pl.when(x + d < X)
        def _(d=d):
            kv_copy(d, x + d).wait_send()

    def drain(k, carry):
        a_copy(k).wait_send()
        for r in range(1, Y):
            b_copy(k, r).wait_send()
        c_copy(k).wait_send()
        c_copy(k).wait_recv()
        return carry

    lax.fori_loop(0, PIECES, drain, 0)


def solution(mesh):
    NP, X, Y = mesh.shape["pipe"], mesh.shape["ctx"] // 2, mesh.shape["tp"] // 2

    def on_device(inputs, doc_lengths, w_query, w_key, w_value, w_out):
        TR, D = inputs.shape[1:]
        TB = TR * 2 * Y
        RB, QW = w_key.shape[1], w_query.shape[2]
        G, NCH, CW = QW // HD, RB // ROWS, D // PIECES
        half = np.arange(HD // 2, dtype=np.float32) * np.float32(2.0) / np.float32(HD)
        freq = np.power(np.float32(ROPE_BASE), -half).astype(np.float32)
        freq = jnp.asarray(np.tile(np.concatenate([freq, freq])[None], (8, 1)))
        bf, f32 = jnp.bfloat16, jnp.float32
        vmem, dma = pltpu.VMEM, pltpu.SemaphoreType.DMA
        hbm = pl.BlockSpec(memory_space=pl.ANY)
        out = pl.pallas_call(
            functools.partial(layer_kernel, (NP, X, Y)),
            out_shape=jax.ShapeDtypeStruct((TR, D), bf),
            in_specs=[
                hbm,
                pl.BlockSpec(memory_space=pltpu.SMEM),
                pl.BlockSpec(memory_space=pltpu.VMEM),
                hbm, hbm, hbm, hbm,
            ],
            out_specs=hbm,
            scratch_shapes=[
                vmem((TB, D), bf), vmem((D, QW), bf), vmem((QW, D), bf), vmem((D, HD), bf), vmem((D, HD), bf),
                vmem((TB, QW), f32), vmem((G * TB, HD), bf), vmem((2, TB, HD), f32), vmem((X, 2, TB, HD), bf),
                vmem((X, TB, TB), f32), vmem((TB, HD), f32), vmem((TB, HD), f32), vmem((G * TB, 2 * HD), f32),
                vmem((TB, QW), bf),
                vmem((PIECES, 2, Y, TR, CW), bf), vmem((PIECES, Y, TR, CW), bf), vmem((PIECES, Y, TR, CW), bf),
                vmem((PIECES, Y - 1, TR, CW), bf), vmem((PIECES, TR, CW), bf),
                dma((5,)), dma((NCH, 2)), dma((NCH, 2)), dma((2 * Y - 1,)), dma((2 * Y - 1,)),
                dma((X - 1, 2)), dma((X - 1, 2)), dma((NCH, X - 1, 2)), dma((NCH, X - 1, 2)),
                dma((X - 1,)), dma((X - 1,)),
                dma((PIECES,)), dma((PIECES,)), dma((PIECES, Y - 1)), dma((PIECES, Y - 1)),
                dma((PIECES,)), dma((PIECES,)),
            ],
            compiler_params=pltpu.CompilerParams(
                collective_id=0, has_side_effects=True, vmem_limit_bytes=56 * 1024 * 1024
            ),
            name="attention_layer",
        )(inputs[0], doc_lengths, freq, w_query[0], w_key[0], w_value[0], w_out[0])
        return out[None]

    in_specs = (
        P("pipe", ("ctx", "tp"), None),
        P("pipe", None),
        P("pipe", None, "tp"),
        P("pipe", "ctx", "tp"),
        P("pipe", "ctx", "tp"),
        P("pipe", "tp", None),
    )
    out_specs = P("pipe", ("ctx", "tp"), None)
    return jax.shard_map(
        on_device, mesh=mesh, in_specs=in_specs, out_specs=out_specs, check_vma=False
    )
```

```python
import functools

import jax
import jax.numpy as jnp
import numpy as np
from jax import lax
from jax.experimental import pallas as pl
from jax.experimental.pallas import tpu as pltpu
from jax.sharding import PartitionSpec as P

HD = 128
ROPE_BASE = 500000.0
NORM_EPS = 1e-06
ROWS = 128
PIECES = 8
NEG = -1e30
LAG = 2
WIN = 2
MESH = pl.DeviceIdType.MESH


def layer_kernel(
    sizes,
    x_ref, len_ref, freq_ref, wq_ref, wk_ref, wv_ref, wo_ref,
    o_ref,
    tok, wq, wo, wk, wv, q_acc, qr, kv_acc, kvb, mask, cosb, sinb, acc, att,
    part, recv_a, pair, recv_b, outb,
    l_sem, z_s, z_r, t_s, t_r, own_s, own_r, fwd_s, fwd_r, kv_s, kv_r,
    a_s, a_r, b_s, b_r, c_s, c_r,
):
    NP, X, Y = sizes
    TP = 2 * Y
    TR, D = x_ref.shape
    TB = TR * TP
    RB = wk_ref.shape[0]
    QW = wq_ref.shape[1]
    G = QW // HD
    NCH = RB // ROWS
    CW = D // PIECES

    pipe, ctx, t = lax.axis_index("pipe"), lax.axis_index("ctx"), lax.axis_index("tp")
    zhi, x = ctx // X, ctx % X
    y, c = t // 2, t % 2

    z_dev = (pipe, (1 - zhi) * X + x, t)
    next_dev = ((pipe + 1) % NP, ctx, t)
    prev_dev = ((pipe + NP - 1) % NP, ctx, t)
    core_dev = (pipe, ctx, y * 2 + 1 - c)

    def flip(i, r, n):
        out = 0
        bit = 1
        while bit < n:
            b = (i // bit) % 2
            out = out + bit * ((1 - b) if (r // bit) % 2 else b)
            bit *= 2
        return out

    def x_dev(xx):
        return (pipe, zhi * X + xx, t)

    def copy(src, dst, ss, rs, dev):
        return pltpu.make_async_remote_copy(
            src_ref=src, dst_ref=dst, send_sem=ss, recv_sem=rs, device_id=dev, device_id_type=MESH
        )

    def rows(start, n):
        return pl.ds(pl.multiple_of(start, n), n)

    mine = ctx * RB
    theirs = ((1 - zhi) * X + x) * RB

    locals_ = [
        pltpu.make_async_copy(x_ref, tok.at[rows(t * TR, TR)], l_sem.at[0]),
        pltpu.make_async_copy(wk_ref, wk.at[rows(mine, ROWS * NCH)], l_sem.at[1]),
        pltpu.make_async_copy(wv_ref, wv.at[rows(mine, ROWS * NCH)], l_sem.at[2]),
        pltpu.make_async_copy(wq_ref, wq, l_sem.at[3]),
        pltpu.make_async_copy(wo_ref, wo, l_sem.at[4]),
    ]
    for cp in locals_:
        cp.start()

    barrier = pltpu.get_barrier_semaphore()
    friends = [z_dev, next_dev, prev_dev]
    friends += [x_dev(flip(x, r, X)) for r in range(1, X)]
    friends += [(pipe, ctx, flip(t, r, TP)) for r in range(1, TP)]
    for dev in friends:
        pl.semaphore_signal(barrier, inc=1, device_id=dev, device_id_type=MESH)
    pl.semaphore_wait(barrier, len(friends))

    def z_copy(j, i, base):
        src = (wk_ref, wv_ref)[i].at[pl.ds(j * ROWS, ROWS)]
        dst = (wk, wv)[i].at[rows(base + j * ROWS, ROWS)]
        return copy(src, dst, z_s.at[j, i], z_r.at[j, i], z_dev)

    for j in range(WIN):
        for i in range(2):
            z_copy(j, i, mine).start()

    def z_next(j):
        if 0 <= j < NCH - WIN:
            for i in range(2):
                z_copy(j, i, mine).wait_send()
                z_copy(j + WIN, i, mine).start()

    def tok_copy(r, who):
        return copy(x_ref, tok.at[rows(who * TR, TR)], t_s.at[r - 1], t_r.at[r - 1], (pipe, ctx, flip(t, r, TP)))

    for r in range(1, TP):
        tok_copy(r, t).start()

    def own_copy(r, i, xx):
        dst = (wk, wv)[i].at[rows((zhi * X + xx) * RB, ROWS * NCH)]
        return copy((wk_ref, wv_ref)[i], dst, own_s.at[r - 1, i], own_r.at[r - 1, i], x_dev(flip(x, r, X)))

    for r in range(1, X):
        for i in range(2):
            own_copy(r, i, x).start()

    first = ctx * TB
    row_pos = lax.broadcasted_iota(jnp.int32, (TB, HD), 0) + first
    angle = row_pos.astype(jnp.float32) * freq_ref[0:1, :]
    cosb[...] = jnp.cos(angle)
    lane = lax.broadcasted_iota(jnp.int32, (TB, HD), 1)
    sine = jnp.sin(angle)
    sinb[...] = jnp.where(lane < HD // 2, -sine, sine)

    n_docs = len_ref.shape[1]
    ends = []
    total = 0
    for m in range(n_docs):
        total = total + len_ref[0, m]
        ends.append(total)
    q_pos = lax.broadcasted_iota(jnp.int32, (TB, TB), 0) + first
    q_doc = sum((q_pos >= e).astype(jnp.int32) for e in ends)
    for d in range(X):
        k_pos = lax.broadcasted_iota(jnp.int32, (TB, TB), 1) + (first - d * TB)
        k_doc = sum((k_pos >= e).astype(jnp.int32) for e in ends)
        mask[d] = jnp.where((k_pos <= q_pos) & (k_doc == q_doc), 0.0, NEG)

    def norm_rotate(head):
        scaled = head * lax.rsqrt(jnp.mean(head * head, axis=-1, keepdims=True) + NORM_EPS)
        return (scaled * cosb[...] + pltpu.roll(scaled, HD // 2, 1) * sinb[...]).astype(jnp.bfloat16)

    for j in range(4 - WIN):
        z_next(j)
    locals_[0].wait()
    for r in range(1, TP):
        tok_copy(r, flip(t, r, TP)).wait_recv()
    locals_[3].wait()
    q_acc[...] = jnp.zeros_like(q_acc)
    QK = D // (2 * X)

    def q_step(i, carry):
        s = rows(i * QK, QK)
        q_acc[...] += jnp.dot(tok[:, s], wq[s, :], preferred_element_type=jnp.float32)
        return carry

    lax.fori_loop(0, 2 * X, q_step, 0)
    for h in range(G):
        qr[pl.ds(h * TB, TB), :] = norm_rotate(q_acc[:, h * HD : (h + 1) * HD])

    locals_[1].wait()
    locals_[2].wait()
    for r in range(1, X):
        for i in range(2):
            own_copy(r, i, flip(x, r, X)).wait_recv()
    kv_acc[...] = jnp.zeros_like(kv_acc)

    def kv_step(i, carry):
        s = rows((zhi * X + i) * RB, ROWS * NCH)
        right = jnp.concatenate([wk[s, :], wv[s, :]], axis=1)
        kv_acc[...] += jnp.dot(tok[:, s], right, preferred_element_type=jnp.float32)
        return carry

    lax.fori_loop(0, X, kv_step, 0)

    def fwd_copy(j, r, i, base):
        ref = (wk, wv)[i].at[rows(base + j * ROWS, ROWS)]
        return copy(ref, ref, fwd_s.at[j, r - 1, i], fwd_r.at[j, r - 1, i], x_dev(flip(x, r, X)))

    def peer_base(r):
        return ((1 - zhi) * X + flip(x, r, X)) * RB

    def cols_of(xx, j):
        return rows(((1 - zhi) * X + xx) * RB + j * ROWS, ROWS)

    def take_chunk(j):
        for r in range(1, X):
            for i in range(2):
                fwd_copy(j, r, i, peer_base(r)).wait_recv()
        left = jnp.concatenate([tok[:, cols_of(r, j)] for r in range(X)], axis=1)
        right = jnp.concatenate(
            [jnp.concatenate([w[cols_of(r, j), :] for r in range(X)], axis=0) for w in (wk, wv)], axis=1
        )
        kv_acc[...] += jnp.dot(left, right, preferred_element_type=jnp.float32)

    for j in range(NCH):
        z_next(4 - WIN + j)
        for i in range(2):
            z_copy(j, i, theirs).wait_recv()
        for r in range(1, X):
            for i in range(2):
                fwd_copy(j, r, i, theirs).start()
        if j and j < NCH - 1:
            take_chunk(j - 1)
    take_chunk(NCH - 2)
    take_chunk(NCH - 1)

    kvb[0, 0] = norm_rotate(kv_acc[:, :HD])
    kvb[0, 1] = kv_acc[:, HD:].astype(jnp.bfloat16)

    def kv_copy(d, xx):
        return copy(kvb.at[0], kvb.at[d], kv_s.at[d - 1], kv_r.at[d - 1], x_dev(xx))

    for d in range(1, X):

        @pl.when(x + d < X)
        def _(d=d):
            kv_copy(d, x + d).start()

    scale = 1.0 / HD**0.5
    ones = jnp.ones((TB, HD), jnp.bfloat16)

    def attend(d):
        s = lax.dot_general(
            qr[...], kvb[d, 0], (((1,), (1,)), ((), ())), preferred_element_type=jnp.float32
        )
        s = s.reshape(G, TB, TB) * scale + mask[d][None]
        e = jnp.exp(s).astype(jnp.bfloat16).reshape(G * TB, TB)
        return jnp.dot(
            e, jnp.concatenate([kvb[d, 1], ones], axis=1), preferred_element_type=jnp.float32
        )

    acc[...] = attend(0)
    for d in range(1, X):

        @pl.when(x >= d)
        def _(d=d):
            kv_copy(d, x - d).wait_recv()
            acc[...] += attend(d)

    for h in range(G):
        block = acc[pl.ds(h * TB, TB), :]
        att[:, h * HD : (h + 1) * HD] = (block[:, :HD] / block[:, HD:]).astype(jnp.bfloat16)

    locals_[4].wait()

    def a_copy(k):
        return copy(part.at[k, 1 - c], recv_a.at[k], a_s.at[k], a_r.at[k], core_dev)

    def b_copy(k, r):
        yy = flip(y, r, Y)
        return copy(pair.at[k, yy], recv_b.at[k, r - 1], b_s.at[k, r - 1], b_r.at[k, r - 1], (pipe, ctx, yy * 2 + c))

    def c_copy(k):
        return copy(outb.at[k], o_ref.at[:, rows(k * CW, CW)], c_s.at[k], c_r.at[k], next_dev)

    def project(k, carry):
        product = jnp.dot(
            att[...], wo[:, rows(k * CW, CW)], preferred_element_type=jnp.float32
        ).astype(jnp.bfloat16)
        for who in range(TP):
            part[k, who % 2, who // 2] = product[who * TR : (who + 1) * TR]
        a_copy(k).start()
        return carry

    def pair_sum(k, carry):
        a_copy(k).wait_recv()
        pair[k] = (part[k, c].astype(jnp.float32) + recv_a[k].astype(jnp.float32)).astype(jnp.bfloat16)
        for r in range(Y - 1, 0, -1):
            b_copy(k, r).start()
        return carry

    lax.fori_loop(0, LAG, project, 0)
    lax.fori_loop(LAG, PIECES, lambda k, carry: pair_sum(k - LAG, project(k, carry)), 0)
    lax.fori_loop(PIECES - LAG, PIECES, pair_sum, 0)

    def last_sum(k, carry):
        whole = part[k, c, y].astype(jnp.float32) + recv_a[k, y].astype(jnp.float32)
        for r in range(1, Y):
            b_copy(k, r).wait_recv()
            whole = whole + recv_b[k, r - 1].astype(jnp.float32)
        outb[k] = whole.astype(jnp.bfloat16)
        c_copy(k).start()
        return carry

    lax.fori_loop(0, PIECES, last_sum, 0)

    for j in range(NCH):
        for i in range(2):
            if j >= NCH - WIN:
                z_copy(j, i, mine).wait_send()
            for r in range(1, X):
                fwd_copy(j, r, i, theirs).wait_send()
    for r in range(1, TP):
        tok_copy(r, t).wait_send()
    for r in range(1, X):
        for i in range(2):
            own_copy(r, i, x).wait_send()
    for d in range(1, X):

        @pl.when(x + d < X)
        def _(d=d):
            kv_copy(d, x + d).wait_send()

    def drain(k, carry):
        a_copy(k).wait_send()
        for r in range(1, Y):
            b_copy(k, r).wait_send()
        c_copy(k).wait_send()
        c_copy(k).wait_recv()
        return carry

    lax.fori_loop(0, PIECES, drain, 0)


def solution(mesh):
    NP, X, Y = mesh.shape["pipe"], mesh.shape["ctx"] // 2, mesh.shape["tp"] // 2

    def on_device(inputs, doc_lengths, w_query, w_key, w_value, w_out):
        TR, D = inputs.shape[1:]
        TB = TR * 2 * Y
        RB, QW = w_key.shape[1], w_query.shape[2]
        G, NCH, CW = QW // HD, RB // ROWS, D // PIECES
        half = np.arange(HD // 2, dtype=np.float32) * np.float32(2.0) / np.float32(HD)
        freq = np.power(np.float32(ROPE_BASE), -half).astype(np.float32)
        freq = jnp.asarray(np.tile(np.concatenate([freq, freq])[None], (8, 1)))
        bf, f32 = jnp.bfloat16, jnp.float32
        vmem, dma = pltpu.VMEM, pltpu.SemaphoreType.DMA
        hbm = pl.BlockSpec(memory_space=pl.ANY)
        out = pl.pallas_call(
            functools.partial(layer_kernel, (NP, X, Y)),
            out_shape=jax.ShapeDtypeStruct((TR, D), bf),
            in_specs=[
                hbm,
                pl.BlockSpec(memory_space=pltpu.SMEM),
                pl.BlockSpec(memory_space=pltpu.VMEM),
                hbm, hbm, hbm, hbm,
            ],
            out_specs=hbm,
            scratch_shapes=[
                vmem((TB, D), bf), vmem((D, QW), bf), vmem((QW, D), bf), vmem((D, HD), bf), vmem((D, HD), bf),
                vmem((TB, QW), f32), vmem((G * TB, HD), bf), vmem((TB, 2 * HD), f32), vmem((X, 2, TB, HD), bf),
                vmem((X, TB, TB), f32), vmem((TB, HD), f32), vmem((TB, HD), f32), vmem((G * TB, 2 * HD), f32),
                vmem((TB, QW), bf),
                vmem((PIECES, 2, Y, TR, CW), bf), vmem((PIECES, Y, TR, CW), bf), vmem((PIECES, Y, TR, CW), bf),
                vmem((PIECES, Y - 1, TR, CW), bf), vmem((PIECES, TR, CW), bf),
                dma((5,)), dma((NCH, 2)), dma((NCH, 2)), dma((2 * Y - 1,)), dma((2 * Y - 1,)),
                dma((X - 1, 2)), dma((X - 1, 2)), dma((NCH, X - 1, 2)), dma((NCH, X - 1, 2)),
                dma((X - 1,)), dma((X - 1,)),
                dma((PIECES,)), dma((PIECES,)), dma((PIECES, Y - 1)), dma((PIECES, Y - 1)),
                dma((PIECES,)), dma((PIECES,)),
            ],
            compiler_params=pltpu.CompilerParams(
                collective_id=0, has_side_effects=True, vmem_limit_bytes=56 * 1024 * 1024
            ),
            name="attention_layer",
        )(inputs[0], doc_lengths, freq, w_query[0], w_key[0], w_value[0], w_out[0])
        return out[None]

    in_specs = (
        P("pipe", ("ctx", "tp"), None),
        P("pipe", None),
        P("pipe", None, "tp"),
        P("pipe", "ctx", "tp"),
        P("pipe", "ctx", "tp"),
        P("pipe", "tp", None),
    )
    out_specs = P("pipe", ("ctx", "tp"), None)
    return jax.shard_map(
        on_device, mesh=mesh, in_specs=in_specs, out_specs=out_specs, check_vma=False
    )
```

```python
import functools

import jax
import jax.numpy as jnp
import numpy as np
from jax import lax
from jax.experimental import pallas as pl
from jax.experimental.pallas import tpu as pltpu
from jax.sharding import PartitionSpec as P

HD = 128
ROPE_BASE = 500000.0
NORM_EPS = 1e-06
ROWS = 128
PIECES = 8
NEG = -1e30
LAG = 2
WIN = 2
MESH = pl.DeviceIdType.MESH


def layer_kernel(
    sizes,
    x_ref, len_ref, freq_ref, wq_ref, wk_ref, wv_ref, wo_ref,
    o_ref,
    tok, wq, wo, wk, wv, q_acc, qr, kv_acc, kvb, mask, cosb, sinb, acc, att,
    part, recv_a, pair, recv_b, half, outb,
    l_sem, z_s, z_r, t_s, t_r, own_s, own_r, fwd_s, fwd_r, kv_s, kv_r,
    a_s, a_r, b_s, b_r, c_s, c_r,
):
    NP, X, Y = sizes
    TP = 2 * Y
    TR, D = x_ref.shape
    TB = TR * TP
    RB = wk_ref.shape[0]
    QW = wq_ref.shape[1]
    G = QW // HD
    NCH = RB // ROWS
    CW = D // PIECES

    pipe, ctx, t = lax.axis_index("pipe"), lax.axis_index("ctx"), lax.axis_index("tp")
    zhi, x = ctx // X, ctx % X
    y, c = t // 2, t % 2

    z_dev = (pipe, (1 - zhi) * X + x, t)
    next_dev = ((pipe + 1) % NP, ctx, t)
    prev_dev = ((pipe + NP - 1) % NP, ctx, t)
    core_dev = (pipe, ctx, y * 2 + 1 - c)

    def flip(i, r, n):
        out = 0
        bit = 1
        while bit < n:
            b = (i // bit) % 2
            out = out + bit * ((1 - b) if (r // bit) % 2 else b)
            bit *= 2
        return out

    def x_dev(xx):
        return (pipe, zhi * X + xx, t)

    def copy(src, dst, ss, rs, dev):
        return pltpu.make_async_remote_copy(
            src_ref=src, dst_ref=dst, send_sem=ss, recv_sem=rs, device_id=dev, device_id_type=MESH
        )

    def rows(start, n):
        return pl.ds(pl.multiple_of(start, n), n)

    mine = ctx * RB
    theirs = ((1 - zhi) * X + x) * RB

    locals_ = [
        pltpu.make_async_copy(x_ref, tok.at[rows(t * TR, TR)], l_sem.at[0]),
        pltpu.make_async_copy(wk_ref, wk.at[rows(mine, ROWS * NCH)], l_sem.at[1]),
        pltpu.make_async_copy(wv_ref, wv.at[rows(mine, ROWS * NCH)], l_sem.at[2]),
        pltpu.make_async_copy(wq_ref, wq, l_sem.at[3]),
        pltpu.make_async_copy(wo_ref, wo, l_sem.at[4]),
    ]
    for cp in locals_:
        cp.start()

    barrier = pltpu.get_barrier_semaphore()
    friends = [z_dev, next_dev, prev_dev]
    friends += [x_dev(flip(x, r, X)) for r in range(1, X)]
    friends += [(pipe, ctx, flip(t, r, TP)) for r in range(1, TP)]
    for dev in friends:
        pl.semaphore_signal(barrier, inc=1, device_id=dev, device_id_type=MESH)
    pl.semaphore_wait(barrier, len(friends))

    def z_copy(j, i, base):
        src = (wk_ref, wv_ref)[i].at[pl.ds(j * ROWS, ROWS)]
        dst = (wk, wv)[i].at[rows(base + j * ROWS, ROWS)]
        return copy(src, dst, z_s.at[j, i], z_r.at[j, i], z_dev)

    for j in range(WIN):
        for i in range(2):
            z_copy(j, i, mine).start()

    def z_next(j):
        if 0 <= j < NCH - WIN:
            for i in range(2):
                z_copy(j, i, mine).wait_send()
                z_copy(j + WIN, i, mine).start()

    def tok_copy(r, who):
        return copy(x_ref, tok.at[rows(who * TR, TR)], t_s.at[r - 1], t_r.at[r - 1], (pipe, ctx, flip(t, r, TP)))

    for r in range(1, TP):
        tok_copy(r, t).start()

    def own_copy(r, i, xx):
        dst = (wk, wv)[i].at[rows((zhi * X + xx) * RB, ROWS * NCH)]
        return copy((wk_ref, wv_ref)[i], dst, own_s.at[r - 1, i], own_r.at[r - 1, i], x_dev(flip(x, r, X)))

    for r in range(1, X):
        for i in range(2):
            own_copy(r, i, x).start()

    first = ctx * TB
    row_pos = lax.broadcasted_iota(jnp.int32, (TB, HD), 0) + first
    angle = row_pos.astype(jnp.float32) * freq_ref[0:1, :]
    cosb[...] = jnp.cos(angle)
    lane = lax.broadcasted_iota(jnp.int32, (TB, HD), 1)
    sine = jnp.sin(angle)
    sinb[...] = jnp.where(lane < HD // 2, -sine, sine)

    n_docs = len_ref.shape[1]
    ends = []
    total = 0
    for m in range(n_docs):
        total = total + len_ref[0, m]
        ends.append(total)
    q_pos = lax.broadcasted_iota(jnp.int32, (TB, TB), 0) + first
    q_doc = sum((q_pos >= e).astype(jnp.int32) for e in ends)
    for d in range(X):
        k_pos = lax.broadcasted_iota(jnp.int32, (TB, TB), 1) + (first - d * TB)
        k_doc = sum((k_pos >= e).astype(jnp.int32) for e in ends)
        mask[d] = jnp.where((k_pos <= q_pos) & (k_doc == q_doc), 0.0, NEG)

    def norm_rotate(head):
        scaled = head * lax.rsqrt(jnp.mean(head * head, axis=-1, keepdims=True) + NORM_EPS)
        return (scaled * cosb[...] + pltpu.roll(scaled, HD // 2, 1) * sinb[...]).astype(jnp.bfloat16)

    for j in range(4 - WIN):
        z_next(j)
    locals_[0].wait()
    for r in range(1, TP):
        tok_copy(r, flip(t, r, TP)).wait_recv()
    locals_[3].wait()
    q_acc[...] = jnp.zeros_like(q_acc)
    QK = D // (2 * X)

    def q_step(i, carry):
        s = rows(i * QK, QK)
        q_acc[...] += jnp.dot(tok[:, s], wq[s, :], preferred_element_type=jnp.float32)
        return carry

    lax.fori_loop(0, 2 * X, q_step, 0)
    for h in range(G):
        qr[pl.ds(h * TB, TB), :] = norm_rotate(q_acc[:, h * HD : (h + 1) * HD])

    locals_[1].wait()
    locals_[2].wait()
    for r in range(1, X):
        for i in range(2):
            own_copy(r, i, flip(x, r, X)).wait_recv()
    kv_acc[...] = jnp.zeros_like(kv_acc)

    def kv_step(i, carry):
        s = rows((zhi * X + i) * RB, ROWS * NCH)
        right = jnp.concatenate([wk[s, :], wv[s, :]], axis=1)
        kv_acc[...] += jnp.dot(tok[:, s], right, preferred_element_type=jnp.float32)
        return carry

    lax.fori_loop(0, X, kv_step, 0)

    def fwd_copy(j, r, i, base):
        ref = (wk, wv)[i].at[rows(base + j * ROWS, ROWS)]
        return copy(ref, ref, fwd_s.at[j, r - 1, i], fwd_r.at[j, r - 1, i], x_dev(flip(x, r, X)))

    def peer_base(r):
        return ((1 - zhi) * X + flip(x, r, X)) * RB

    def cols_of(xx, j):
        return rows(((1 - zhi) * X + xx) * RB + j * ROWS, ROWS)

    def take_chunk(j):
        for r in range(1, X):
            for i in range(2):
                fwd_copy(j, r, i, peer_base(r)).wait_recv()
        left = jnp.concatenate([tok[:, cols_of(r, j)] for r in range(X)], axis=1)
        right = jnp.concatenate(
            [jnp.concatenate([w[cols_of(r, j), :] for r in range(X)], axis=0) for w in (wk, wv)], axis=1
        )
        kv_acc[...] += jnp.dot(left, right, preferred_element_type=jnp.float32)

    for j in range(NCH):
        z_next(4 - WIN + j)
        for i in range(2):
            z_copy(j, i, theirs).wait_recv()
        for r in range(1, X):
            for i in range(2):
                fwd_copy(j, r, i, theirs).start()
        if j and j < NCH - 1:
            take_chunk(j - 1)
    take_chunk(NCH - 2)
    take_chunk(NCH - 1)

    kvb[0, 0] = norm_rotate(kv_acc[:, :HD])
    kvb[0, 1] = kv_acc[:, HD:].astype(jnp.bfloat16)

    def kv_copy(d, xx):
        return copy(kvb.at[0], kvb.at[d], kv_s.at[d - 1], kv_r.at[d - 1], x_dev(xx))

    for d in range(1, X):

        @pl.when(x + d < X)
        def _(d=d):
            kv_copy(d, x + d).start()

    scale = 1.0 / HD**0.5
    ones = jnp.ones((TB, HD), jnp.bfloat16)

    def attend(d):
        s = lax.dot_general(
            qr[...], kvb[d, 0], (((1,), (1,)), ((), ())), preferred_element_type=jnp.float32
        )
        s = s.reshape(G, TB, TB) * scale + mask[d][None]
        e = jnp.exp(s).astype(jnp.bfloat16).reshape(G * TB, TB)
        return jnp.dot(
            e, jnp.concatenate([kvb[d, 1], ones], axis=1), preferred_element_type=jnp.float32
        )

    acc[...] = attend(0)
    for d in range(1, X):

        @pl.when(x >= d)
        def _(d=d):
            kv_copy(d, x - d).wait_recv()
            acc[...] += attend(d)

    for h in range(G):
        block = acc[pl.ds(h * TB, TB), :]
        att[:, h * HD : (h + 1) * HD] = (block[:, :HD] / block[:, HD:]).astype(jnp.bfloat16)

    locals_[4].wait()

    def a_copy(k):
        return copy(part.at[k, 1 - c], recv_a.at[k], a_s.at[k], a_r.at[k], core_dev)

    near, far = flip(y, 1, Y), flip(y, 3, Y)

    def first_of(k):
        return near + (far - near) * (k % 2)

    def second_of(k):
        return far + (near - far) * (k % 2)

    def b_copy(k, r):
        to = first_of(k)
        which = flip(y, 2, Y) if r else to
        return copy(pair.at[k, which], recv_b.at[k, r], b_s.at[k, r], b_r.at[k, r], (pipe, ctx, to * 2 + c))

    def h_copy(k):
        return copy(half.at[k], recv_b.at[k, 2], b_s.at[k, 2], b_r.at[k, 2], (pipe, ctx, second_of(k) * 2 + c))

    def c_copy(k):
        return copy(outb.at[k], o_ref.at[:, rows(k * CW, CW)], c_s.at[k], c_r.at[k], next_dev)

    def project(k, carry):
        product = jnp.dot(
            att[...], wo[:, rows(k * CW, CW)], preferred_element_type=jnp.float32
        ).astype(jnp.bfloat16)
        for who in range(TP):
            part[k, who % 2, who // 2] = product[who * TR : (who + 1) * TR]
        a_copy(k).start()
        return carry

    def pair_sum(k, carry):
        a_copy(k).wait_recv()
        pair[k] = (part[k, c].astype(jnp.float32) + recv_a[k].astype(jnp.float32)).astype(jnp.bfloat16)
        b_copy(k, 1).start()
        b_copy(k, 0).start()
        return carry

    def half_sum(k, carry):
        b_copy(k, 1).wait_recv()
        to = second_of(k)
        mid = part[k, c, to].astype(jnp.float32) + recv_a[k, to].astype(jnp.float32)
        half[k] = (mid + recv_b[k, 1].astype(jnp.float32)).astype(jnp.bfloat16)
        h_copy(k).start()
        return carry

    lax.fori_loop(0, LAG, project, 0)
    lax.fori_loop(LAG, PIECES, lambda k, carry: pair_sum(k - LAG, project(k, carry)), 0)
    lax.fori_loop(PIECES - LAG, PIECES, pair_sum, 0)

    def last_sum(k, carry):
        whole = part[k, c, y].astype(jnp.float32) + recv_a[k, y].astype(jnp.float32)
        b_copy(k, 0).wait_recv()
        h_copy(k).wait_recv()
        whole = whole + recv_b[k, 0].astype(jnp.float32) + recv_b[k, 2].astype(jnp.float32)
        outb[k] = whole.astype(jnp.bfloat16)
        c_copy(k).start()
        return carry

    lax.fori_loop(0, LAG, half_sum, 0)
    lax.fori_loop(LAG, PIECES, lambda k, carry: last_sum(k - LAG, half_sum(k, carry)), 0)
    lax.fori_loop(PIECES - LAG, PIECES, last_sum, 0)

    for j in range(NCH):
        for i in range(2):
            if j >= NCH - WIN:
                z_copy(j, i, mine).wait_send()
            for r in range(1, X):
                fwd_copy(j, r, i, theirs).wait_send()
    for r in range(1, TP):
        tok_copy(r, t).wait_send()
    for r in range(1, X):
        for i in range(2):
            own_copy(r, i, x).wait_send()
    for d in range(1, X):

        @pl.when(x + d < X)
        def _(d=d):
            kv_copy(d, x + d).wait_send()

    def drain(k, carry):
        a_copy(k).wait_send()
        b_copy(k, 0).wait_send()
        b_copy(k, 1).wait_send()
        h_copy(k).wait_send()
        c_copy(k).wait_send()
        c_copy(k).wait_recv()
        return carry

    lax.fori_loop(0, PIECES, drain, 0)


def solution(mesh):
    NP, X, Y = mesh.shape["pipe"], mesh.shape["ctx"] // 2, mesh.shape["tp"] // 2

    def on_device(inputs, doc_lengths, w_query, w_key, w_value, w_out):
        TR, D = inputs.shape[1:]
        TB = TR * 2 * Y
        RB, QW = w_key.shape[1], w_query.shape[2]
        G, NCH, CW = QW // HD, RB // ROWS, D // PIECES
        half = np.arange(HD // 2, dtype=np.float32) * np.float32(2.0) / np.float32(HD)
        freq = np.power(np.float32(ROPE_BASE), -half).astype(np.float32)
        freq = jnp.asarray(np.tile(np.concatenate([freq, freq])[None], (8, 1)))
        bf, f32 = jnp.bfloat16, jnp.float32
        vmem, dma = pltpu.VMEM, pltpu.SemaphoreType.DMA
        hbm = pl.BlockSpec(memory_space=pl.ANY)
        out = pl.pallas_call(
            functools.partial(layer_kernel, (NP, X, Y)),
            out_shape=jax.ShapeDtypeStruct((TR, D), bf),
            in_specs=[
                hbm,
                pl.BlockSpec(memory_space=pltpu.SMEM),
                pl.BlockSpec(memory_space=pltpu.VMEM),
                hbm, hbm, hbm, hbm,
            ],
            out_specs=hbm,
            scratch_shapes=[
                vmem((TB, D), bf), vmem((D, QW), bf), vmem((QW, D), bf), vmem((D, HD), bf), vmem((D, HD), bf),
                vmem((TB, QW), f32), vmem((G * TB, HD), bf), vmem((TB, 2 * HD), f32), vmem((X, 2, TB, HD), bf),
                vmem((X, TB, TB), f32), vmem((TB, HD), f32), vmem((TB, HD), f32), vmem((G * TB, 2 * HD), f32),
                vmem((TB, QW), bf),
                vmem((PIECES, 2, Y, TR, CW), bf), vmem((PIECES, Y, TR, CW), bf), vmem((PIECES, Y, TR, CW), bf),
                vmem((PIECES, Y - 1, TR, CW), bf), vmem((PIECES, TR, CW), bf), vmem((PIECES, TR, CW), bf),
                dma((5,)), dma((NCH, 2)), dma((NCH, 2)), dma((2 * Y - 1,)), dma((2 * Y - 1,)),
                dma((X - 1, 2)), dma((X - 1, 2)), dma((NCH, X - 1, 2)), dma((NCH, X - 1, 2)),
                dma((X - 1,)), dma((X - 1,)),
                dma((PIECES,)), dma((PIECES,)), dma((PIECES, Y - 1)), dma((PIECES, Y - 1)),
                dma((PIECES,)), dma((PIECES,)),
            ],
            compiler_params=pltpu.CompilerParams(
                collective_id=0, has_side_effects=True, vmem_limit_bytes=56 * 1024 * 1024
            ),
            name="attention_layer",
        )(inputs[0], doc_lengths, freq, w_query[0], w_key[0], w_value[0], w_out[0])
        return out[None]

    in_specs = (
        P("pipe", ("ctx", "tp"), None),
        P("pipe", None),
        P("pipe", None, "tp"),
        P("pipe", "ctx", "tp"),
        P("pipe", "ctx", "tp"),
        P("pipe", "tp", None),
    )
    out_specs = P("pipe", ("ctx", "tp"), None)
    return jax.shard_map(
        on_device, mesh=mesh, in_specs=in_specs, out_specs=out_specs, check_vma=False
    )
```

```python
import functools

import jax
import jax.numpy as jnp
import numpy as np
from jax import lax
from jax.experimental import pallas as pl
from jax.experimental.pallas import tpu as pltpu
from jax.sharding import PartitionSpec as P

HD = 128
ROPE_BASE = 500000.0
NORM_EPS = 1e-06
ROWS = 128
PIECES = 8
NEG = -1e30
LAG = 2
WIN = 2
MESH = pl.DeviceIdType.MESH


def layer_kernel(
    sizes,
    x_ref, len_ref, freq_ref, wq_ref, wk_ref, wv_ref, wo_ref,
    o_ref,
    tok, wq, wo, wk, wv, q_acc, qr, kv_acc, kvb, mask, cosb, sinb, acc, att,
    part, recv_a, pair, recv_b, outb,
    l_sem, z_s, z_r, t_s, t_r, own_s, own_r, fwd_s, fwd_r, kv_s, kv_r,
    a_s, a_r, b_s, b_r, c_s, c_r,
):
    NP, X, Y = sizes
    TP = 2 * Y
    TR, D = x_ref.shape
    TB = TR * TP
    RB = wk_ref.shape[0]
    QW = wq_ref.shape[1]
    G = QW // HD
    NCH = RB // ROWS
    CW = D // PIECES

    pipe, ctx, t = lax.axis_index("pipe"), lax.axis_index("ctx"), lax.axis_index("tp")
    zhi, x = ctx // X, ctx % X
    y, c = t // 2, t % 2

    z_dev = (pipe, (1 - zhi) * X + x, t)
    next_dev = ((pipe + 1) % NP, ctx, t)
    prev_dev = ((pipe + NP - 1) % NP, ctx, t)
    core_dev = (pipe, ctx, y * 2 + 1 - c)

    def flip(i, r, n):
        out = 0
        bit = 1
        while bit < n:
            b = (i // bit) % 2
            out = out + bit * ((1 - b) if (r // bit) % 2 else b)
            bit *= 2
        return out

    def x_dev(xx):
        return (pipe, zhi * X + xx, t)

    def copy(src, dst, ss, rs, dev):
        return pltpu.make_async_remote_copy(
            src_ref=src, dst_ref=dst, send_sem=ss, recv_sem=rs, device_id=dev, device_id_type=MESH
        )

    def rows(start, n):
        return pl.ds(pl.multiple_of(start, n), n)

    mine = ctx * RB
    theirs = ((1 - zhi) * X + x) * RB

    locals_ = [
        pltpu.make_async_copy(x_ref, tok.at[rows(t * TR, TR)], l_sem.at[0]),
        pltpu.make_async_copy(wk_ref, wk.at[rows(mine, ROWS * NCH)], l_sem.at[1]),
        pltpu.make_async_copy(wv_ref, wv.at[rows(mine, ROWS * NCH)], l_sem.at[2]),
        pltpu.make_async_copy(wq_ref, wq, l_sem.at[3]),
        pltpu.make_async_copy(wo_ref, wo, l_sem.at[4]),
    ]
    for cp in locals_:
        cp.start()

    barrier = pltpu.get_barrier_semaphore()
    friends = [z_dev, next_dev, prev_dev]
    friends += [x_dev(flip(x, r, X)) for r in range(1, X)]
    friends += [(pipe, ctx, flip(t, r, TP)) for r in range(1, TP)]
    for dev in friends:
        pl.semaphore_signal(barrier, inc=1, device_id=dev, device_id_type=MESH)
    pl.semaphore_wait(barrier, len(friends))

    def z_copy(j, i, base):
        src = (wk_ref, wv_ref)[i].at[pl.ds(j * ROWS, ROWS)]
        dst = (wk, wv)[i].at[rows(base + j * ROWS, ROWS)]
        return copy(src, dst, z_s.at[j, i], z_r.at[j, i], z_dev)

    for j in range(WIN):
        for i in range(2):
            z_copy(j, i, mine).start()

    def z_next(j):
        if 0 <= j < NCH - WIN:
            for i in range(2):
                z_copy(j, i, mine).wait_send()
                z_copy(j + WIN, i, mine).start()

    def tok_copy(r, who):
        return copy(x_ref, tok.at[rows(who * TR, TR)], t_s.at[r - 1], t_r.at[r - 1], (pipe, ctx, flip(t, r, TP)))

    for r in range(1, TP):
        tok_copy(r, t).start()

    def own_copy(r, i, xx):
        dst = (wk, wv)[i].at[rows((zhi * X + xx) * RB, ROWS * NCH)]
        return copy((wk_ref, wv_ref)[i], dst, own_s.at[r - 1, i], own_r.at[r - 1, i], x_dev(flip(x, r, X)))

    for r in range(1, X):
        for i in range(2):
            own_copy(r, i, x).start()

    first = ctx * TB
    row_pos = lax.broadcasted_iota(jnp.int32, (TB, HD), 0) + first
    angle = row_pos.astype(jnp.float32) * freq_ref[0:1, :]
    cosb[...] = jnp.cos(angle)
    lane = lax.broadcasted_iota(jnp.int32, (TB, HD), 1)
    sine = jnp.sin(angle)
    sinb[...] = jnp.where(lane < HD // 2, -sine, sine)

    n_docs = len_ref.shape[1]
    ends = []
    total = 0
    for m in range(n_docs):
        total = total + len_ref[0, m]
        ends.append(total)
    q_pos = lax.broadcasted_iota(jnp.int32, (TB, TB), 0) + first
    q_doc = sum((q_pos >= e).astype(jnp.int32) for e in ends)
    for d in range(X):
        k_pos = lax.broadcasted_iota(jnp.int32, (TB, TB), 1) + (first - d * TB)
        k_doc = sum((k_pos >= e).astype(jnp.int32) for e in ends)
        mask[d] = jnp.where((k_pos <= q_pos) & (k_doc == q_doc), 0.0, NEG)

    def norm_rotate(head):
        scaled = head * lax.rsqrt(jnp.mean(head * head, axis=-1, keepdims=True) + NORM_EPS)
        return (scaled * cosb[...] + pltpu.roll(scaled, HD // 2, 1) * sinb[...]).astype(jnp.bfloat16)

    for j in range(4 - WIN):
        z_next(j)
    locals_[0].wait()
    for r in range(1, TP):
        tok_copy(r, flip(t, r, TP)).wait_recv()
    locals_[3].wait()
    q_acc[...] = jnp.zeros_like(q_acc)
    QK = D // (2 * X)

    def q_step(i, carry):
        s = rows(i * QK, QK)
        q_acc[...] += jnp.dot(tok[:, s], wq[s, :], preferred_element_type=jnp.float32)
        return carry

    lax.fori_loop(0, 2 * X, q_step, 0)
    for h in range(G):
        qr[pl.ds(h * TB, TB), :] = norm_rotate(q_acc[:, h * HD : (h + 1) * HD])

    locals_[1].wait()
    locals_[2].wait()
    for r in range(1, X):
        for i in range(2):
            own_copy(r, i, flip(x, r, X)).wait_recv()
    kv_acc[...] = jnp.zeros_like(kv_acc)

    def kv_step(i, carry):
        s = rows((zhi * X + i) * RB, ROWS * NCH)
        right = jnp.concatenate([wk[s, :], wv[s, :]], axis=1)
        kv_acc[...] += jnp.dot(tok[:, s], right, preferred_element_type=jnp.float32)
        return carry

    lax.fori_loop(0, X, kv_step, 0)

    def fwd_copy(j, r, i, base):
        ref = (wk, wv)[i].at[rows(base + j * ROWS, ROWS)]
        return copy(ref, ref, fwd_s.at[j, r - 1, i], fwd_r.at[j, r - 1, i], x_dev(flip(x, r, X)))

    def peer_base(r):
        return ((1 - zhi) * X + flip(x, r, X)) * RB

    def cols_of(xx, j):
        return rows(((1 - zhi) * X + xx) * RB + j * ROWS, ROWS)

    def take_chunk(j):
        for r in range(1, X):
            for i in range(2):
                fwd_copy(j, r, i, peer_base(r)).wait_recv()
        left = jnp.concatenate([tok[:, cols_of(r, j)] for r in range(X)], axis=1)
        right = jnp.concatenate(
            [jnp.concatenate([w[cols_of(r, j), :] for r in range(X)], axis=0) for w in (wk, wv)], axis=1
        )
        kv_acc[...] += jnp.dot(left, right, preferred_element_type=jnp.float32)

    for j in range(NCH):
        z_next(4 - WIN + j)
        for i in range(2):
            z_copy(j, i, theirs).wait_recv()
        for r in range(1, X):
            for i in range(2):
                fwd_copy(j, r, i, theirs).start()
        if j and j < NCH - 1:
            take_chunk(j - 1)
    take_chunk(NCH - 2)
    take_chunk(NCH - 1)

    kvb[0, 0] = norm_rotate(kv_acc[:, :HD])
    kvb[0, 1] = kv_acc[:, HD:].astype(jnp.bfloat16)

    def kv_copy(d, xx):
        return copy(kvb.at[0], kvb.at[d], kv_s.at[d - 1], kv_r.at[d - 1], x_dev(xx))

    for d in range(1, X):

        @pl.when(x + d < X)
        def _(d=d):
            kv_copy(d, x + d).start()

    scale = 1.0 / HD**0.5
    ones = jnp.ones((TB, HD), jnp.bfloat16)

    def attend(d):
        s = lax.dot_general(
            qr[...], kvb[d, 0], (((1,), (1,)), ((), ())), preferred_element_type=jnp.float32
        )
        s = s.reshape(G, TB, TB) * scale + mask[d][None]
        e = jnp.exp(s).astype(jnp.bfloat16).reshape(G * TB, TB)
        return jnp.dot(
            e, jnp.concatenate([kvb[d, 1], ones], axis=1), preferred_element_type=jnp.float32
        )

    acc[...] = attend(0)
    for d in range(1, X):

        @pl.when(x >= d)
        def _(d=d):
            kv_copy(d, x - d).wait_recv()
            acc[...] += attend(d)

    for h in range(G):
        block = acc[pl.ds(h * TB, TB), :]
        att[:, h * HD : (h + 1) * HD] = (block[:, :HD] / block[:, HD:]).astype(jnp.bfloat16)

    locals_[4].wait()

    def a_copy(k):
        return copy(part.at[k, 1 - c], recv_a.at[k], a_s.at[k], a_r.at[k], core_dev)

    def b_copy(k, r):
        yy = flip(y, r, Y)
        return copy(pair.at[k, yy], recv_b.at[k, r - 1], b_s.at[k, r - 1], b_r.at[k, r - 1], (pipe, ctx, yy * 2 + c))

    def c_copy(k):
        return copy(outb.at[k], o_ref.at[:, rows(k * CW, CW)], c_s.at[k], c_r.at[k], next_dev)

    def project(k, carry):
        product = jnp.dot(
            att[...], wo[:, rows(k * CW, CW)], preferred_element_type=jnp.float32
        ).astype(jnp.bfloat16)
        for who in range(TP):
            part[k, who % 2, who // 2] = product[who * TR : (who + 1) * TR]
        a_copy(k).start()
        return carry

    def pair_sum(k, carry):
        a_copy(k).wait_recv()
        pair[k] = (part[k, c].astype(jnp.float32) + recv_a[k].astype(jnp.float32)).astype(jnp.bfloat16)
        for r in range(Y - 1, 0, -1):
            b_copy(k, r).start()
        return carry

    lax.fori_loop(0, LAG, project, 0)
    lax.fori_loop(LAG, PIECES, lambda k, carry: pair_sum(k - LAG, project(k, carry)), 0)
    lax.fori_loop(PIECES - LAG, PIECES, pair_sum, 0)

    def last_sum(k, carry):
        whole = part[k, c, y].astype(jnp.float32) + recv_a[k, y].astype(jnp.float32)
        for r in range(1, Y):
            b_copy(k, r).wait_recv()
            whole = whole + recv_b[k, r - 1].astype(jnp.float32)
        outb[k] = whole.astype(jnp.bfloat16)
        c_copy(k).start()
        return carry

    lax.fori_loop(0, PIECES, last_sum, 0)

    for j in range(NCH):
        for i in range(2):
            if j >= NCH - WIN:
                z_copy(j, i, mine).wait_send()
            for r in range(1, X):
                fwd_copy(j, r, i, theirs).wait_send()
    for r in range(1, TP):
        tok_copy(r, t).wait_send()
    for r in range(1, X):
        for i in range(2):
            own_copy(r, i, x).wait_send()
    for d in range(1, X):

        @pl.when(x + d < X)
        def _(d=d):
            kv_copy(d, x + d).wait_send()

    def drain(k, carry):
        a_copy(k).wait_send()
        for r in range(1, Y):
            b_copy(k, r).wait_send()
        c_copy(k).wait_send()
        c_copy(k).wait_recv()
        return carry

    lax.fori_loop(0, PIECES, drain, 0)


def deliver(src_ref, dst_ref, held, in_sem, out_sem):
    BR = 8
    count = src_ref.shape[0] // BR
    taken = [
        pltpu.make_async_copy(src_ref.at[pl.ds(i * BR, BR)], held.at[i], in_sem.at[i]) for i in range(count)
    ]
    given = [
        pltpu.make_async_copy(held.at[i], dst_ref.at[pl.ds(i * BR, BR)], out_sem.at[i]) for i in range(count)
    ]
    for cp in taken:
        cp.start()
    for i in range(count):
        taken[i].wait()
        given[i].start()
    for cp in given:
        cp.wait()


def solution(mesh):
    NP, X, Y = mesh.shape["pipe"], mesh.shape["ctx"] // 2, mesh.shape["tp"] // 2

    def on_device(inputs, doc_lengths, w_query, w_key, w_value, w_out):
        TR, D = inputs.shape[1:]
        TB = TR * 2 * Y
        RB, QW = w_key.shape[1], w_query.shape[2]
        G, NCH, CW = QW // HD, RB // ROWS, D // PIECES
        half = np.arange(HD // 2, dtype=np.float32) * np.float32(2.0) / np.float32(HD)
        freq = np.power(np.float32(ROPE_BASE), -half).astype(np.float32)
        freq = jnp.asarray(np.tile(np.concatenate([freq, freq])[None], (8, 1)))
        bf, f32 = jnp.bfloat16, jnp.float32
        vmem, dma = pltpu.VMEM, pltpu.SemaphoreType.DMA
        hbm = pl.BlockSpec(memory_space=pl.ANY)
        out = pl.pallas_call(
            functools.partial(layer_kernel, (NP, X, Y)),
            out_shape=jax.ShapeDtypeStruct((TR, D), bf),
            in_specs=[
                hbm,
                pl.BlockSpec(memory_space=pltpu.SMEM),
                pl.BlockSpec(memory_space=pltpu.VMEM),
                hbm, hbm, hbm, hbm,
            ],
            out_specs=hbm,
            scratch_shapes=[
                vmem((TB, D), bf), vmem((D, QW), bf), vmem((QW, D), bf), vmem((D, HD), bf), vmem((D, HD), bf),
                vmem((TB, QW), f32), vmem((G * TB, HD), bf), vmem((TB, 2 * HD), f32), vmem((X, 2, TB, HD), bf),
                vmem((X, TB, TB), f32), vmem((TB, HD), f32), vmem((TB, HD), f32), vmem((G * TB, 2 * HD), f32),
                vmem((TB, QW), bf),
                vmem((PIECES, 2, Y, TR, CW), bf), vmem((PIECES, Y, TR, CW), bf), vmem((PIECES, Y, TR, CW), bf),
                vmem((PIECES, Y - 1, TR, CW), bf), vmem((PIECES, TR, CW), bf),
                dma((5,)), dma((NCH, 2)), dma((NCH, 2)), dma((2 * Y - 1,)), dma((2 * Y - 1,)),
                dma((X - 1, 2)), dma((X - 1, 2)), dma((NCH, X - 1, 2)), dma((NCH, X - 1, 2)),
                dma((X - 1,)), dma((X - 1,)),
                dma((PIECES,)), dma((PIECES,)), dma((PIECES, Y - 1)), dma((PIECES, Y - 1)),
                dma((PIECES,)), dma((PIECES,)),
            ],
            compiler_params=pltpu.CompilerParams(
                collective_id=0, has_side_effects=True, vmem_limit_bytes=56 * 1024 * 1024
            ),
            name="attention_layer",
        )(inputs[0], doc_lengths, freq, w_query[0], w_key[0], w_value[0], w_out[0])
        out = pl.pallas_call(
            deliver,
            out_shape=jax.ShapeDtypeStruct((TR, D), bf),
            in_specs=[hbm],
            out_specs=hbm,
            scratch_shapes=[vmem((TR // 8, 8, D), bf), dma((TR // 8,)), dma((TR // 8,))],
            name="deliver",
        )(out)
        return out[None]

    in_specs = (
        P("pipe", ("ctx", "tp"), None),
        P("pipe", None),
        P("pipe", None, "tp"),
        P("pipe", "ctx", "tp"),
        P("pipe", "ctx", "tp"),
        P("pipe", "tp", None),
    )
    out_specs = P("pipe", ("ctx", "tp"), None)
    return jax.shard_map(
        on_device, mesh=mesh, in_specs=in_specs, out_specs=out_specs, check_vma=False
    )
```
